32 devices in a mesh: groups: 1, chain: 4 (over y, x), tm: 8 (over z, core).
Axes of the slice: x: 2, y: 2, z: 4, core: 2. Of those that a mesh axis runs over, the one named last changes fastest.
Arguments:
- traces: bfloat16 [4, 2048, 1024], P(('groups', 'chain'), 'tm'), may hold values from -100 to 100
- lengths: int32 [4], P('groups'), may hold values from 1024 to 1793, as said below
Outputs:
- omega: float32 [1024, 1024], P(('groups', 'chain', 'tm'))
The draws below stay inside these ranges and needn't reach their ends.
Inputs may be any that keep to these rules, and one draw needn't show every extreme that they name: `lengths`: every chain has between half of the window and 1793 valid draws; some chain has exactly each of the two ends.
All inputs are finite; a program needn't handle non-finite values.
Results may differ from the reference program's by a relative error of at most 0.0003.
Values may be sent and summed in bfloat16 or wider, within the bound.
A program may use at most 64 MiB of HBM per device.

```python
import math
import jax
import jax.numpy as jnp
from jax import lax

P_SIZE = 1024
LAG = 256
CHAINS = 4
TIME = 2048


def draw_traces(key, part):
    key_scale = jax.random.fold_in(key, 11)
    key_noise = jax.random.fold_in(key, 12)
    key_level = jax.random.fold_in(key, 13)
    key_sign = jax.random.fold_in(key, 14)
    spread = jnp.exp(jax.random.uniform(key_scale, (P_SIZE,), jnp.float32, 0.0, math.log(10.0)))
    noise = jnp.clip(jax.random.normal(key_noise, (CHAINS, TIME, P_SIZE), jnp.float32), -6.0, 6.0)
    level = jax.random.uniform(key_level, (CHAINS, 1, P_SIZE), jnp.float32, 1.0, 3.0)
    sign = jnp.where(jax.random.uniform(key_sign, (CHAINS, 1, P_SIZE), jnp.float32) < 0.5, -1.0, 1.0)
    ramp = 0.5 + jnp.arange(TIME).astype(jnp.float32) / TIME
    values = level * sign * ramp[None, :, None] + spread[None, None, :] * noise
    return values.astype(jnp.bfloat16)


def draw_lengths(key, part):
    key_body = jax.random.fold_in(key, 21)
    key_first = jax.random.fold_in(key, 22)
    key_second = jax.random.fold_in(key, 23)
    values = jax.random.randint(key_body, (CHAINS,), TIME // 2, TIME - LAG + 2, jnp.int32)
    first = jax.random.randint(key_first, (), 0, CHAINS, jnp.int32)
    offset = jax.random.randint(key_second, (), 1, CHAINS, jnp.int32)
    second = (first + offset) % CHAINS
    index = jnp.arange(CHAINS, dtype=jnp.int32)
    values = jnp.where(index == first, TIME - LAG + 1, values)
    values = jnp.where(index == second, TIME // 2, values)
    return values.astype(jnp.int32)


def setup_inputs(seed: int = 0, part: int = 0) -> dict:
    seeds = jax.random.split(jax.random.key(seed), 3)
    part_splits = jax.random.split(jax.random.fold_in(seeds[2], part), 3)
    traces = draw_traces(jax.random.fold_in(jax.random.fold_in(seeds[2], part), 71), part)
    lengths = draw_lengths(jax.random.fold_in(jax.random.fold_in(seeds[2], part), 71), part)
    return {"traces": traces, "lengths": lengths}


def window_sums(current, previous):
    chains, steps, width = current.shape
    count = steps // LAG
    blocks = current.reshape(chains, count, LAG, width)
    earlier = jnp.concatenate([previous[:, None], blocks[:, :-1]], axis=1)
    index = jnp.arange(LAG)
    lower = (index[None, :] <= index[:, None]).astype(jnp.float32)
    upper = (index[None, :] > index[:, None]).astype(jnp.float32)
    result = jnp.einsum("ij,cbjp->cbip", lower, blocks, precision=lax.Precision.HIGHEST)
    result = result + jnp.einsum("ij,cbjp->cbip", upper, earlier, precision=lax.Precision.HIGHEST)
    return result.reshape(chains, steps, width)


def reference(traces, lengths):
    def one_chain(total, item):
        trace, length = item
        valid = (jnp.arange(TIME) < length).astype(jnp.float32)[:, None]
        data = trace.astype(jnp.float32) * valid
        mean = jnp.sum(data, axis=0) / length.astype(jnp.float32)
        centered = (data - mean[None, :]) * valid
        filtered = window_sums(centered[None], jnp.zeros((1, LAG, P_SIZE), jnp.float32))[0]
        product = jnp.einsum("tk,tp->kp", filtered, filtered, precision=lax.Precision.HIGHEST)
        return total + product, None

    start = jnp.zeros((P_SIZE, P_SIZE), jnp.float32)
    total, _ = lax.scan(one_chain, start, (traces, lengths))
    scale = 1.0 / (LAG * jnp.sum(lengths).astype(jnp.float32))
    return total * scale
```

```python
import functools

import jax
import jax.numpy as jnp
from jax import lax
from jax.experimental import pallas as pl
from jax.experimental.pallas import tpu as pltpu
from jax.sharding import PartitionSpec as P

LAG = 256
MESH = pl.DeviceIdType.MESH


def shifted(block, axis, distance):
    devices = range(lax.axis_size(axis))
    route = [(i - distance, i) for i in devices if i - distance in devices]
    return lax.ppermute(block, axis, route)


def window_sums(current, previous):
    chains, steps, width = current.shape
    count = steps // LAG
    blocks = current.reshape(chains, count, LAG, width)
    earlier = jnp.concatenate([previous[:, None], blocks[:, :-1]], axis=1)
    index = jnp.arange(LAG)
    lower = index[None, :] <= index[:, None]
    upper = index[None, :] > index[:, None]
    lower_mat = lower.astype(jnp.float32)
    upper_mat = upper.astype(jnp.float32)
    result = jnp.einsum("ij,cbjp->cbip", lower_mat, blocks, precision=lax.Precision.HIGHEST)
    result = result + jnp.einsum(
        "ij,cbjp->cbip", upper_mat, earlier, precision=lax.Precision.HIGHEST
    )
    return result.reshape(chains, steps, width)


def gram_rows(filtered):
    chains, steps, width = filtered.shape
    flat = filtered.reshape(chains * steps, width)
    return jnp.einsum("tk,tp->kp", flat, flat, precision=lax.Precision.HIGHEST)


def on_device(traces, lengths):
    chains, steps, width = traces.shape
    own_len = lax.dynamic_slice_in_dim(lengths, lax.axis_index("chain") * chains, chains)
    first_time = lax.axis_index("tm") * steps
    times = first_time + jnp.arange(steps, dtype=jnp.int32)
    valid = (times[None, :] < own_len[:, None]).astype(jnp.float32)
    back_times = times - steps
    back_valid = ((back_times[None, :] >= 0) & (back_times[None, :] < own_len[:, None])).astype(
        jnp.float32
    )
    behind = shifted(traces, "tm", 1)
    data = traces.astype(jnp.float32) * valid[..., None]
    earlier = behind.astype(jnp.float32) * back_valid[..., None]
    totals = lax.psum(jnp.sum(data, axis=1), "tm")
    mean = totals / own_len.astype(jnp.float32)[:, None]
    scale = 1.0 / (LAG * jnp.sum(lengths).astype(jnp.float32))
    centered = window_sums(
        (data - mean[:, None, :]) * valid[..., None],
        (earlier - mean[:, None, :]) * back_valid[..., None],
    )
    return lax.psum_scatter(
        scale * gram_rows(centered), ("chain", "tm"), scatter_dimension=0, tiled=True
    )


def dot(a, b):
    return jnp.dot(a, b, preferred_element_type=jnp.float32)


NQ = 4


def kernel(
    len_ref, x_ref, o_ref, data, sums, hi, lo, hi_t, lo_t, gram, part1, part2, plane, lines,
    done, other, s_sum, r_sum, s_x, r_x, s_halo, r_halo, s_fwd, r_fwd, s1, r1, s2, r2, s3, r3,
    s4, r4,
):
    steps, width = x_ref.shape
    half = width // 2
    cols = half // NQ
    rows = width // 4
    zrows = rows // 4
    orows = zrows // 2
    c = lax.axis_index("chain")
    k = lax.axis_index("tm")
    z = k // 2
    j = k % 2

    def copy(src, dst, send, recv, **where):
        return pltpu.make_async_remote_copy(
            src_ref=src, dst_ref=dst, send_sem=send, recv_sem=recv, device_id=where,
            device_id_type=MESH,
        )

    barrier = pltpu.get_barrier_semaphore()
    for r in range(1, 8):
        pl.semaphore_signal(barrier, inc=1, device_id={"tm": k ^ r}, device_id_type=MESH)
    for r in (1, 2):
        pl.semaphore_signal(barrier, inc=1, device_id={"chain": c ^ r}, device_id_type=MESH)

    length = len_ref[c]
    total_len = len_ref[0]
    for i in range(1, len_ref.shape[0]):
        total_len = total_len + len_ref[i]
    scale = 1.0 / (LAG * jnp.full((1, 1), total_len, jnp.int32).astype(jnp.float32))

    time = k * steps + lax.broadcasted_iota(jnp.int32, (steps, 1), 0)
    valid = (time < length).astype(jnp.float32)
    sums[0] = jnp.sum(x_ref[...].astype(jnp.float32) * valid, axis=0, keepdims=True)
    own = pl.ds(pl.multiple_of(steps + steps * j, steps), steps)
    data[own, :] = x_ref[...]

    @pl.when(z == 0)
    def _():
        data[0:steps, :] = jnp.zeros((steps, width), data.dtype)

    pl.semaphore_wait(barrier, 9)

    sum_copies = [
        copy(sums.at[0], sums.at[r], s_sum.at[r], r_sum.at[r], tm=k ^ r) for r in range(1, 8)
    ]
    for cp in sum_copies:
        cp.start()
    halo_copies = [
        copy(
            x_ref.at[:, pl.ds(half * h, half)],
            data.at[pl.ds(0, steps), pl.ds(half * h, half)],
            s_halo.at[h], r_halo, tm=2 * jnp.minimum(z + 1, 3) + h,
        )
        for h in range(2)
    ]

    @pl.when((j == 1) & (z < 3))
    def _():
        for cp in halo_copies:
            cp.start()

    x_copy = copy(x_ref, data.at[own, :], s_x, r_x, tm=k ^ 1)
    x_copy.start()

    i_idx = lax.broadcasted_iota(jnp.int32, (steps, 2 * steps), 0)
    r_idx = lax.broadcasted_iota(jnp.int32, (steps, 2 * steps), 1)
    for cp in sum_copies:
        cp.wait_recv()
    total = sums[0]
    for r in range(1, 8):
        total = total + sums[r]
    mean = total / jnp.full((1, 1), length, jnp.int32).astype(jnp.float32)

    def windows(b):
        first = 2 * steps * z + steps * b
        when = first - steps + r_idx
        keep = (r_idx > i_idx) & (r_idx <= i_idx + LAG) & (when >= 0) & (when < length)
        band = keep.astype(jnp.float32).astype(jnp.bfloat16)
        t = first + lax.broadcasted_iota(jnp.int32, (steps, 1), 0)
        count = jnp.maximum(
            jnp.minimum(t + 1, length) - jnp.maximum(t - (LAG - 1), 0), 0
        ).astype(jnp.float32)
        out = slice(steps * b, steps * (b + 1))
        for n in range(width // 256):
            at = slice(256 * n, 256 * (n + 1))
            w = dot(band, data[steps * b : steps * (b + 2), at]) - count * mean[:, at]
            h = w.astype(jnp.bfloat16)
            e = (w - h.astype(jnp.float32)).astype(jnp.bfloat16)
            hi[out, at] = h
            lo[out, at] = e
            hi_t[at, out] = h.T
            lo_t[at, out] = e.T

    x_copy.wait_recv()
    windows(1)
    mine = pl.ds(pl.multiple_of(half * j, half), half)
    forward = copy(
        data.at[pl.ds(0, steps), mine], data.at[pl.ds(0, steps), mine], s_fwd, r_fwd, tm=k ^ 1
    )

    @pl.when(z > 0)
    def _():
        copy(
            x_ref.at[:, pl.ds(0, half)], data.at[pl.ds(0, steps), mine], s_halo.at[0], r_halo,
            tm=k ^ 1,
        ).wait_recv()
        forward.start()
        forward.wait_recv()

    windows(0)

    first_hop, second_hop, z_hops, swaps = [], [], [], []
    for q in range(NQ):
        m1 = 1 + q % 2
        m2 = 3 - m1
        first_hop.append([
            copy(gram.at[q, m1], part1.at[q, 0], s1.at[q, 0], r1.at[q, 0], chain=c ^ m1),
            copy(gram.at[q, 3], part1.at[q, 1], s1.at[q, 1], r1.at[q, 1], chain=c ^ m1),
        ])
        second_hop.append(copy(gram.at[q, m2], part2.at[q], s2.at[q], r2.at[q], chain=c ^ m2))
        z_hops.append([
            copy(
                plane.at[q, pl.ds(pl.multiple_of(zrows * (z ^ s), zrows), zrows), :],
                lines.at[q, s - 1], s3.at[q, s - 1], r3.at[q, s - 1], tm=k ^ (2 * s),
            )
            for s in range(1, 4)
        ])
        swaps.append(
            copy(
                done.at[q, pl.ds(pl.multiple_of(orows * (1 - j), orows), orows), :],
                other.at[q], s4.at[q], r4.at[q], tm=k ^ 1,
            )
        )

    def hop2(q):
        m2 = 2 - q % 2
        first_hop[q][1].wait_recv()
        gram[q, m2] = gram[q, m2] + part1[q, 1]
        second_hop[q].start()

    def hop3(q):
        first_hop[q][0].wait_recv()
        second_hop[q].wait_recv()
        plane[q] = gram[q, 0] + part1[q, 0] + part2[q]
        for cp in z_hops[q]:
            cp.start()

    def hop4(q):
        here = plane[q, pl.ds(pl.multiple_of(zrows * z, zrows), zrows), :]
        for s in range(3):
            z_hops[q][s].wait_recv()
            here = here + lines[q, s]
        done[q] = here * scale
        swaps[q].start()

    for p in range(NQ // 2):
        at = pl.ds(pl.multiple_of(half * j + 2 * cols * p, 2 * cols), 2 * cols)
        right_hi = hi[:, at]
        right_lo = lo[:, at]
        for r in (3, 1, 2, 0):
            left = pl.ds(pl.multiple_of(rows * (c ^ r), rows), rows)
            g = (
                dot(hi_t[left, :], right_lo)
                + dot(lo_t[left, :], right_hi)
                + dot(hi_t[left, :], right_hi)
            )
            for b in range(2):
                gram[2 * p + b, r] = g[:, cols * b : cols * (b + 1)]
            if r == 3:
                first_hop[2 * p][1].start()
                first_hop[2 * p + 1][1].start()
            elif r:
                first_hop[2 * p + r - 1][0].start()

    for q in range(NQ):
        hop2(q)
    for q in range(NQ):
        hop3(q)
    for q in range(NQ):
        hop4(q)
    for q in range(NQ):
        o_ref[:, pl.ds(pl.multiple_of(half * j + cols * q, cols), cols)] = done[
            q, pl.ds(pl.multiple_of(orows * j, orows), orows), :
        ]
        swaps[q].wait_recv()
        o_ref[:, pl.ds(pl.multiple_of(half * (1 - j) + cols * q, cols), cols)] = other[q]

    for cp in sum_copies:
        cp.wait_send()
    x_copy.wait_send()

    @pl.when((j == 1) & (z < 3))
    def _():
        for cp in halo_copies:
            cp.wait_send()

    @pl.when(z > 0)
    def _():
        forward.wait_send()

    for q in range(NQ):
        for cp in first_hop[q]:
            cp.wait_send()
        second_hop[q].wait_send()
        for cp in z_hops[q]:
            cp.wait_send()
        swaps[q].wait_send()


def fused(traces, lengths):
    _, steps, width = traces.shape
    f32, bf16 = jnp.float32, jnp.bfloat16
    rows, cols = width // 4, width // 2 // NQ
    dma = pltpu.SemaphoreType.DMA
    return pl.pallas_call(
        kernel,
        out_shape=jax.ShapeDtypeStruct((width // 32, width), f32),
        in_specs=[
            pl.BlockSpec(memory_space=pltpu.SMEM),
            pl.BlockSpec(memory_space=pltpu.VMEM),
        ],
        out_specs=pl.BlockSpec(memory_space=pltpu.VMEM),
        scratch_shapes=[
            pltpu.VMEM((3 * steps, width), bf16),
            pltpu.VMEM((8, 1, width), f32),
            pltpu.VMEM((2 * steps, width), bf16),
            pltpu.VMEM((2 * steps, width), bf16),
            pltpu.VMEM((width, 2 * steps), bf16),
            pltpu.VMEM((width, 2 * steps), bf16),
            pltpu.VMEM((NQ, 4, rows, cols), f32),
            pltpu.VMEM((NQ, 2, rows, cols), f32),
            pltpu.VMEM((NQ, rows, cols), f32),
            pltpu.VMEM((NQ, rows, cols), f32),
            pltpu.VMEM((NQ, 3, rows // 4, cols), f32),
            pltpu.VMEM((NQ, rows // 4, cols), f32),
            pltpu.VMEM((NQ, rows // 8, cols), f32),
            dma((8,)), dma((8,)),
            dma, dma,
            dma((2,)), dma,
            dma, dma,
            dma((NQ, 2)), dma((NQ, 2)),
            dma((NQ,)), dma((NQ,)),
            dma((NQ, 3)), dma((NQ, 3)),
            dma((NQ,)), dma((NQ,)),
        ],
        compiler_params=pltpu.CompilerParams(
            collective_id=0, has_side_effects=True, vmem_limit_bytes=48 * 1024 * 1024
        ),
    )(lengths, traces.reshape(steps, width))


def body(mesh, traces, lengths):
    chains, steps, width = traces.shape
    laid_out = (
        mesh.shape["groups"] == 1 and mesh.shape["chain"] == 4 and mesh.shape["tm"] == 8
    )
    if laid_out and chains == 1 and steps == LAG and width % 1024 == 0:
        return fused(traces, lengths)
    return on_device(traces, lengths)


def solution(mesh):
    in_specs = (P(("groups", "chain"), "tm", None), P("groups"))
    out_specs = P(("groups", "chain", "tm"), None)
    return jax.shard_map(
        functools.partial(body, mesh), mesh=mesh, in_specs=in_specs, out_specs=out_specs,
        check_vma=False,
    )
```

```python
import functools

import jax
import jax.numpy as jnp
from jax import lax
from jax.experimental import pallas as pl
from jax.experimental.pallas import tpu as pltpu
from jax.sharding import PartitionSpec as P

LAG = 256
MESH = pl.DeviceIdType.MESH


def shifted(block, axis, distance):
    devices = range(lax.axis_size(axis))
    route = [(i - distance, i) for i in devices if i - distance in devices]
    return lax.ppermute(block, axis, route)


def window_sums(current, previous):
    chains, steps, width = current.shape
    count = steps // LAG
    blocks = current.reshape(chains, count, LAG, width)
    earlier = jnp.concatenate([previous[:, None], blocks[:, :-1]], axis=1)
    index = jnp.arange(LAG)
    lower = index[None, :] <= index[:, None]
    upper = index[None, :] > index[:, None]
    lower_mat = lower.astype(jnp.float32)
    upper_mat = upper.astype(jnp.float32)
    result = jnp.einsum("ij,cbjp->cbip", lower_mat, blocks, precision=lax.Precision.HIGHEST)
    result = result + jnp.einsum(
        "ij,cbjp->cbip", upper_mat, earlier, precision=lax.Precision.HIGHEST
    )
    return result.reshape(chains, steps, width)


def gram_rows(filtered):
    chains, steps, width = filtered.shape
    flat = filtered.reshape(chains * steps, width)
    return jnp.einsum("tk,tp->kp", flat, flat, precision=lax.Precision.HIGHEST)


def on_device(traces, lengths):
    chains, steps, width = traces.shape
    own_len = lax.dynamic_slice_in_dim(lengths, lax.axis_index("chain") * chains, chains)
    first_time = lax.axis_index("tm") * steps
    times = first_time + jnp.arange(steps, dtype=jnp.int32)
    valid = (times[None, :] < own_len[:, None]).astype(jnp.float32)
    back_times = times - steps
    back_valid = ((back_times[None, :] >= 0) & (back_times[None, :] < own_len[:, None])).astype(
        jnp.float32
    )
    behind = shifted(traces, "tm", 1)
    data = traces.astype(jnp.float32) * valid[..., None]
    earlier = behind.astype(jnp.float32) * back_valid[..., None]
    totals = lax.psum(jnp.sum(data, axis=1), "tm")
    mean = totals / own_len.astype(jnp.float32)[:, None]
    scale = 1.0 / (LAG * jnp.sum(lengths).astype(jnp.float32))
    centered = window_sums(
        (data - mean[:, None, :]) * valid[..., None],
        (earlier - mean[:, None, :]) * back_valid[..., None],
    )
    return lax.psum_scatter(
        scale * gram_rows(centered), ("chain", "tm"), scatter_dimension=0, tiled=True
    )


def dot(a, b):
    return jnp.dot(a, b, preferred_element_type=jnp.float32)


NQ = 4
TOP = 32767.0


def kernel(
    len_ref, x_ref, o_ref, data, sums, hi, lo, hi_t, lo_t, keep, code1, scale1, got1,
    gots1, code2, scale2, got2, gots2, plane, code3, scale3, got3, gots3, done, other, s_sum, r_sum, s_x, r_x, s_halo, r_halo, s_fwd, r_fwd, s1, r1, s1s,
    r1s, s2, r2, s2s, r2s, s3, r3, s3s, r3s, s4, r4,
):
    steps, width = x_ref.shape
    half = width // 2
    cols = half // NQ
    rows = width // 4
    zrows = rows // 4
    orows = zrows // 2
    c = lax.axis_index("chain")
    k = lax.axis_index("tm")
    z = k // 2
    j = k % 2

    def copy(src, dst, send, recv, **where):
        return pltpu.make_async_remote_copy(
            src_ref=src, dst_ref=dst, send_sem=send, recv_sem=recv, device_id=where,
            device_id_type=MESH,
        )

    barrier = pltpu.get_barrier_semaphore()
    for r in range(1, 8):
        pl.semaphore_signal(barrier, inc=1, device_id={"tm": k ^ r}, device_id_type=MESH)
    for r in (1, 2):
        pl.semaphore_signal(barrier, inc=1, device_id={"chain": c ^ r}, device_id_type=MESH)

    length = len_ref[c]
    total_len = len_ref[0]
    for i in range(1, len_ref.shape[0]):
        total_len = total_len + len_ref[i]
    scale = 1.0 / (LAG * jnp.full((1, 1), total_len, jnp.int32).astype(jnp.float32))

    time = k * steps + lax.broadcasted_iota(jnp.int32, (steps, 1), 0)
    valid = (time < length).astype(jnp.float32)
    sums[0] = jnp.sum(x_ref[...].astype(jnp.float32) * valid, axis=0, keepdims=True)
    own = pl.ds(pl.multiple_of(steps + steps * j, steps), steps)
    data[own, :] = x_ref[...]

    @pl.when(z == 0)
    def _():
        data[0:steps, :] = jnp.zeros((steps, width), data.dtype)

    pl.semaphore_wait(barrier, 9)

    sum_copies = [
        copy(sums.at[0], sums.at[r], s_sum.at[r], r_sum.at[r], tm=k ^ r) for r in range(1, 8)
    ]
    for cp in sum_copies:
        cp.start()
    halo_copies = [
        copy(
            x_ref.at[:, pl.ds(half * h, half)],
            data.at[pl.ds(0, steps), pl.ds(half * h, half)],
            s_halo.at[h], r_halo, tm=2 * jnp.minimum(z + 1, 3) + h,
        )
        for h in range(2)
    ]

    @pl.when((j == 1) & (z < 3))
    def _():
        for cp in halo_copies:
            cp.start()

    x_copy = copy(x_ref, data.at[own, :], s_x, r_x, tm=k ^ 1)
    x_copy.start()

    i_idx = lax.broadcasted_iota(jnp.int32, (steps, 2 * steps), 0)
    r_idx = lax.broadcasted_iota(jnp.int32, (steps, 2 * steps), 1)
    for cp in sum_copies:
        cp.wait_recv()
    total = sums[0]
    for r in range(1, 8):
        total = total + sums[r]
    mean = total / jnp.full((1, 1), length, jnp.int32).astype(jnp.float32)

    def windows(b):
        first = 2 * steps * z + steps * b
        when = first - steps + r_idx
        keep = (r_idx > i_idx) & (r_idx <= i_idx + LAG) & (when >= 0) & (when < length)
        band = keep.astype(jnp.float32).astype(jnp.bfloat16)
        t = first + lax.broadcasted_iota(jnp.int32, (steps, 1), 0)
        count = jnp.maximum(
            jnp.minimum(t + 1, length) - jnp.maximum(t - (LAG - 1), 0), 0
        ).astype(jnp.float32)
        out = slice(steps * b, steps * (b + 1))
        for n in range(width // 256):
            at = slice(256 * n, 256 * (n + 1))
            w = dot(band, data[steps * b : steps * (b + 2), at]) - count * mean[:, at]
            h = w.astype(jnp.bfloat16)
            e = (w - h.astype(jnp.float32)).astype(jnp.bfloat16)
            hi[out, at] = h
            lo[out, at] = e
            hi_t[at, out] = h.T
            lo_t[at, out] = e.T

    x_copy.wait_recv()
    windows(1)
    mine = pl.ds(pl.multiple_of(half * j, half), half)
    forward = copy(
        data.at[pl.ds(0, steps), mine], data.at[pl.ds(0, steps), mine], s_fwd, r_fwd, tm=k ^ 1
    )

    @pl.when(z > 0)
    def _():
        copy(
            x_ref.at[:, pl.ds(0, half)], data.at[pl.ds(0, steps), mine], s_halo.at[0], r_halo,
            tm=k ^ 1,
        ).wait_recv()
        forward.start()
        forward.wait_recv()

    windows(0)

    def send(codes, scales, to_codes, to_scales, sems, at, **where):
        (sc, rc), (ss, rs) = sems
        return [
            copy(codes, to_codes, sc.at[at], rc.at[at], **where),
            copy(scales, to_scales, ss.at[at], rs.at[at], **where),
        ]

    def start(copies):
        for cp in copies:
            cp.start()

    def arrive(copies):
        for cp in copies:
            cp.wait_recv()

    def pack(values, codes, scales, at):
        for g in range(8):
            v = values(g)
            top = jnp.maximum(jnp.max(jnp.abs(v), axis=0, keepdims=True), 1e-33)
            scales[(*at, g // 2, slice(g % 2, g % 2 + 1))] = top * (1.0 / TOP)
            code = jnp.round(v * (TOP / top)).astype(jnp.int32).astype(jnp.int16)
            codes[(*at, slice(32 * g, 32 * g + 32))] = code

    def unpack(codes, scales, at, g, base=None):
        code = codes[(*at, slice(32 * g, 32 * g + 32))].astype(jnp.int32).astype(jnp.float32)
        if base is None:
            return code * scales[(*at, g // 2, slice(g % 2, g % 2 + 1))]
        return code * scales[(*at, slice(g, g + 1))]

    first_hop, second_hop, z_hops, swaps = [], [], [], []
    for q in range(NQ):
        m1 = 1 + q % 2
        m2 = 3 - m1
        first_hop.append([
            send(
                code1.at[q, i], scale1.at[q, i], got1.at[q, i], gots1.at[q, i],
                ((s1, r1), (s1s, r1s)), (q, i), chain=c ^ m1,
            )
            for i in range(2)
        ])
        second_hop.append(
            send(
                code2.at[q], scale2.at[q], got2.at[q], gots2.at[q], ((s2, r2), (s2s, r2s)), q,
                chain=c ^ m2,
            )
        )
        z_hops.append([
            send(
                code3.at[q, pl.ds(pl.multiple_of(zrows * (z ^ s), zrows), zrows), :],
                scale3.at[q, z ^ s], got3.at[q, s - 1], gots3.at[q, s - 1],
                ((s3, r3), (s3s, r3s)), (q, s - 1), tm=k ^ (2 * s),
            )
            for s in range(1, 4)
        ])
        swaps.append(
            copy(
                done.at[q, pl.ds(pl.multiple_of(orows * (1 - j), orows), orows), :],
                other.at[q], s4.at[q], r4.at[q], tm=k ^ 1,
            )
        )

    def hop2(q):
        arrive(first_hop[q][1])
        pack(
            lambda g: keep[q, 1, 32 * g : 32 * g + 32] + unpack(got1, gots1, (q, 1), g),
            code2, scale2, (q,),
        )
        start(second_hop[q])

    def hop3(q):
        arrive(first_hop[q][0])
        arrive(second_hop[q])

        def value(g):
            v = (
                keep[q, 0, 32 * g : 32 * g + 32]
                + unpack(got1, gots1, (q, 0), g)
                + unpack(got2, gots2, (q,), g)
            )
            plane[q, 32 * g : 32 * g + 32] = v
            return v

        pack(value, code3, scale3, (q,))
        for copies in z_hops[q]:
            start(copies)

    def hop4(q):
        for s in range(3):
            arrive(z_hops[q][s])
        for g in range(2):
            at = pl.ds(pl.multiple_of(zrows * z + orows * g, orows), orows)
            here = plane[q, at, :]
            for s in range(3):
                here = here + unpack(got3, gots3, (q, s), g, 0)
            done[q, 32 * g : 32 * g + 32] = here * scale
        swaps[q].start()

    def products(p, go):
        at = pl.ds(pl.multiple_of(half * j + 2 * cols * p, 2 * cols), 2 * cols)
        right_hi = hi[:, at]
        right_lo = lo[:, at]
        for r in (3, 1, 2, 0):
            left = pl.ds(pl.multiple_of(rows * (c ^ r), rows), rows)
            w = (
                dot(hi_t[left, :], right_lo)
                + dot(lo_t[left, :], right_hi)
                + dot(hi_t[left, :], right_hi)
            )
            for b in range(2):
                q = 2 * p + b
                part = w[:, cols * b : cols * (b + 1)]
                if r == 3 or r == 1 + b:
                    slot = int(r == 3)
                    pack(lambda g: part[32 * g : 32 * g + 32], code1, scale1, (q, slot))
                    if go:
                        start(first_hop[q][slot])
                else:
                    keep[q, int(r != 0)] = part

    products(0, True)
    products(1, False)
    hop2(0)
    hop2(1)
    for i in (1, 0):
        start(first_hop[2][i])
        start(first_hop[3][i])
    hop3(0)
    hop3(1)
    hop2(2)
    hop2(3)
    hop3(2)
    hop3(3)
    for q in range(NQ):
        hop4(q)
    for q in range(NQ):
        o_ref[:, pl.ds(pl.multiple_of(half * j + cols * q, cols), cols)] = done[
            q, pl.ds(pl.multiple_of(orows * j, orows), orows), :
        ]
        swaps[q].wait_recv()
        o_ref[:, pl.ds(pl.multiple_of(half * (1 - j) + cols * q, cols), cols)] = other[q]

    for cp in sum_copies:
        cp.wait_send()
    x_copy.wait_send()

    @pl.when((j == 1) & (z < 3))
    def _():
        for cp in halo_copies:
            cp.wait_send()

    @pl.when(z > 0)
    def _():
        forward.wait_send()

    for q in range(NQ):
        for copies in (*first_hop[q], second_hop[q], *z_hops[q]):
            for cp in copies:
                cp.wait_send()
        swaps[q].wait_send()


def fused(traces, lengths):
    _, steps, width = traces.shape
    f32, bf16, i16 = jnp.float32, jnp.bfloat16, jnp.int16
    rows, cols = width // 4, width // 2 // NQ
    dma = pltpu.SemaphoreType.DMA
    return pl.pallas_call(
        kernel,
        out_shape=jax.ShapeDtypeStruct((width // 32, width), f32),
        in_specs=[
            pl.BlockSpec(memory_space=pltpu.SMEM),
            pl.BlockSpec(memory_space=pltpu.VMEM),
        ],
        out_specs=pl.BlockSpec(memory_space=pltpu.VMEM),
        scratch_shapes=[
            pltpu.VMEM((3 * steps, width), bf16),
            pltpu.VMEM((8, 1, width), f32),
            pltpu.VMEM((2 * steps, width), bf16),
            pltpu.VMEM((2 * steps, width), bf16),
            pltpu.VMEM((width, 2 * steps), bf16),
            pltpu.VMEM((width, 2 * steps), bf16),
            pltpu.VMEM((NQ, 2, rows, cols), f32),
            pltpu.VMEM((NQ, 2, rows, cols), i16),
            pltpu.VMEM((NQ, 2, 4, 2, cols), f32),
            pltpu.VMEM((NQ, 2, rows, cols), i16),
            pltpu.VMEM((NQ, 2, 4, 2, cols), f32),
            pltpu.VMEM((NQ, rows, cols), i16),
            pltpu.VMEM((NQ, 4, 2, cols), f32),
            pltpu.VMEM((NQ, rows, cols), i16),
            pltpu.VMEM((NQ, 4, 2, cols), f32),
            pltpu.VMEM((NQ, rows, cols), f32),
            pltpu.VMEM((NQ, rows, cols), i16),
            pltpu.VMEM((NQ, 4, 2, cols), f32),
            pltpu.VMEM((NQ, 3, rows // 4, cols), i16),
            pltpu.VMEM((NQ, 3, 2, cols), f32),
            pltpu.VMEM((NQ, rows // 4, cols), f32),
            pltpu.VMEM((NQ, rows // 8, cols), f32),
            dma((8,)), dma((8,)),
            dma, dma,
            dma((2,)), dma,
            dma, dma,
            dma((NQ, 2)), dma((NQ, 2)), dma((NQ, 2)), dma((NQ, 2)),
            dma((NQ,)), dma((NQ,)), dma((NQ,)), dma((NQ,)),
            dma((NQ, 3)), dma((NQ, 3)), dma((NQ, 3)), dma((NQ, 3)),
            dma((NQ,)), dma((NQ,)),
        ],
        compiler_params=pltpu.CompilerParams(
            collective_id=0, has_side_effects=True, vmem_limit_bytes=48 * 1024 * 1024
        ),
    )(lengths, traces.reshape(steps, width))


def body(mesh, traces, lengths):
    chains, steps, width = traces.shape
    laid_out = (
        mesh.shape["groups"] == 1 and mesh.shape["chain"] == 4 and mesh.shape["tm"] == 8
    )
    if laid_out and chains == 1 and steps == LAG and width == 1024:
        return fused(traces, lengths)
    return on_device(traces, lengths)


def solution(mesh):
    in_specs = (P(("groups", "chain"), "tm", None), P("groups"))
    out_specs = P(("groups", "chain", "tm"), None)
    return jax.shard_map(
        functools.partial(body, mesh), mesh=mesh, in_specs=in_specs, out_specs=out_specs,
        check_vma=False,
    )
```

```python
import functools

import jax
import jax.numpy as jnp
from jax import lax
from jax.experimental import pallas as pl
from jax.experimental.pallas import tpu as pltpu
from jax.sharding import PartitionSpec as P

LAG = 256
MESH = pl.DeviceIdType.MESH


def shifted(block, axis, distance):
    devices = range(lax.axis_size(axis))
    route = [(i - distance, i) for i in devices if i - distance in devices]
    return lax.ppermute(block, axis, route)


def window_sums(current, previous):
    chains, steps, width = current.shape
    count = steps // LAG
    blocks = current.reshape(chains, count, LAG, width)
    earlier = jnp.concatenate([previous[:, None], blocks[:, :-1]], axis=1)
    index = jnp.arange(LAG)
    lower = index[None, :] <= index[:, None]
    upper = index[None, :] > index[:, None]
    lower_mat = lower.astype(jnp.float32)
    upper_mat = upper.astype(jnp.float32)
    result = jnp.einsum("ij,cbjp->cbip", lower_mat, blocks, precision=lax.Precision.HIGHEST)
    result = result + jnp.einsum(
        "ij,cbjp->cbip", upper_mat, earlier, precision=lax.Precision.HIGHEST
    )
    return result.reshape(chains, steps, width)


def gram_rows(filtered):
    chains, steps, width = filtered.shape
    flat = filtered.reshape(chains * steps, width)
    return jnp.einsum("tk,tp->kp", flat, flat, precision=lax.Precision.HIGHEST)


def on_device(traces, lengths):
    chains, steps, width = traces.shape
    own_len = lax.dynamic_slice_in_dim(lengths, lax.axis_index("chain") * chains, chains)
    first_time = lax.axis_index("tm") * steps
    times = first_time + jnp.arange(steps, dtype=jnp.int32)
    valid = (times[None, :] < own_len[:, None]).astype(jnp.float32)
    back_times = times - steps
    back_valid = ((back_times[None, :] >= 0) & (back_times[None, :] < own_len[:, None])).astype(
        jnp.float32
    )
    behind = shifted(traces, "tm", 1)
    data = traces.astype(jnp.float32) * valid[..., None]
    earlier = behind.astype(jnp.float32) * back_valid[..., None]
    totals = lax.psum(jnp.sum(data, axis=1), "tm")
    mean = totals / own_len.astype(jnp.float32)[:, None]
    scale = 1.0 / (LAG * jnp.sum(lengths).astype(jnp.float32))
    centered = window_sums(
        (data - mean[:, None, :]) * valid[..., None],
        (earlier - mean[:, None, :]) * back_valid[..., None],
    )
    return lax.psum_scatter(
        scale * gram_rows(centered), ("chain", "tm"), scatter_dimension=0, tiled=True
    )


def dot(a, b):
    return jnp.dot(a, b, preferred_element_type=jnp.float32)


NQ = 4
TOP = 32767.0


def kernel(
    len_hbm, x_hbm, o_ref, len_ref, data, ext, hi_e, lo_e, hi_et, lo_et, sums, hi, lo, hi_t, lo_t, keep, code1, scale1, got1,
    gots1, code2, scale2, got2, gots2, plane, code3, scale3, got3, gots3, done, other, in_sem, s_sum, r_sum, s_x, r_x,
    s_halo, r_halo, s_fwd, r_fwd, s1, r1, s1s,
    r1s, s2, r2, s2s, r2s, s3, r3, s3s, r3s, s4, r4,
):
    steps, width = x_hbm.shape
    pad = steps // 2
    half = width // 2
    cols = half // NQ
    rows = width // 4
    zrows = rows // 4
    orows = zrows // 2
    c = lax.axis_index("chain")
    k = lax.axis_index("tm")
    z = k // 2
    j = k % 2

    def copy(src, dst, send, recv, **where):
        return pltpu.make_async_remote_copy(
            src_ref=src, dst_ref=dst, send_sem=send, recv_sem=recv, device_id=where,
            device_id_type=MESH,
        )

    def start(copies):
        for cp in copies:
            cp.start()

    def arrive(copies):
        for cp in copies:
            cp.wait_recv()

    own = pl.ds(pl.multiple_of(pad + steps * j, pad), steps)
    len_in = pltpu.make_async_copy(len_hbm, len_ref, in_sem.at[0])
    x_in = pltpu.make_async_copy(x_hbm, data.at[own, :], in_sem.at[1])
    len_in.start()
    x_in.start()
    barrier = pltpu.get_barrier_semaphore()
    for r in range(1, 8):
        pl.semaphore_signal(barrier, inc=1, device_id={"tm": k ^ r}, device_id_type=MESH)
    for r in (1, 2):
        pl.semaphore_signal(barrier, inc=1, device_id={"chain": c ^ r}, device_id_type=MESH)

    len_in.wait()
    length = len_ref[c]
    total_len = len_ref[0]
    for i in range(1, len_ref.shape[0]):
        total_len = total_len + len_ref[i]
    scale = 1.0 / (LAG * jnp.full((1, 1), total_len, jnp.int32).astype(jnp.float32))

    time = k * steps + lax.broadcasted_iota(jnp.int32, (steps, 1), 0)
    valid = (time < length).astype(jnp.float32)
    x_in.wait()
    sums[0] = jnp.sum(data[own, :].astype(jnp.float32) * valid, axis=0, keepdims=True)

    @pl.when(z == 0)
    def _():
        data[0:pad, :] = jnp.zeros((pad, width), data.dtype)

    @pl.when(z == 3)
    def _():
        data[5 * pad : 6 * pad, :] = jnp.zeros((pad, width), data.dtype)

    pl.semaphore_wait(barrier, 9)

    sum_copies = [
        copy(sums.at[0], sums.at[r], s_sum.at[r], r_sum.at[r], tm=k ^ r) for r in range(1, 8)
    ]
    for cp in sum_copies:
        cp.start()
    def halo(way, h):
        near = 2 * jnp.minimum(z + 1, 3) if way == 0 else 2 * jnp.maximum(z - 1, 0)
        take = 4 * pad if way == 0 else pad
        put = 0 if way == 0 else 5 * pad
        at = pl.ds(half * h, half)
        return copy(
            data.at[pl.ds(take, pad), at], data.at[pl.ds(put, pad), at], s_halo.at[h],
            r_halo.at[way], tm=near + h,
        )

    ups = [halo(0, h) for h in range(2)]
    downs = [halo(1, h) for h in range(2)]

    @pl.when((j == 1) & (z < 3))
    def _():
        start(ups)

    @pl.when((j == 0) & (z > 0))
    def _():
        start(downs)

    x_copy = copy(data.at[own, :], data.at[own, :], s_x, r_x, tm=k ^ 1)
    x_copy.start()

    mine = pl.ds(pl.multiple_of(half * j, half), half)
    forwards, landed = [], []
    for way, put in ((0, 0), (1, 5 * pad)):
        block = data.at[pl.ds(put, pad), mine]
        forwards.append(copy(block, block, s_fwd.at[way], r_fwd.at[way], tm=k ^ 1))
        landed.append(copy(block, block, s_halo.at[0], r_halo.at[way], tm=k ^ 1))

    @pl.when(z > 0)
    def _():
        landed[0].wait_recv()
        forwards[0].start()

    @pl.when(z < 3)
    def _():
        landed[1].wait_recv()
        forwards[1].start()

    i_idx = lax.broadcasted_iota(jnp.int32, (steps, 2 * steps), 0)
    r_idx = lax.broadcasted_iota(jnp.int32, (steps, 2 * steps), 1)
    for cp in sum_copies:
        cp.wait_recv()
    total = sums[0]
    for r in range(1, 8):
        total = total + sums[r]
    mean = total / jnp.full((1, 1), length, jnp.int32).astype(jnp.float32)

    def windows(b):
        first = 2 * steps * z + pad + steps * b
        when = first - steps + r_idx
        keep = (r_idx > i_idx) & (r_idx <= i_idx + LAG) & (when >= 0) & (when < length)
        band = keep.astype(jnp.float32).astype(jnp.bfloat16)
        t = first + lax.broadcasted_iota(jnp.int32, (steps, 1), 0)
        count = jnp.maximum(
            jnp.minimum(t + 1, length) - jnp.maximum(t - (LAG - 1), 0), 0
        ).astype(jnp.float32)
        out = slice(steps * b, steps * (b + 1))
        for n in range(width // 256):
            at = slice(256 * n, 256 * (n + 1))
            w = dot(band, data[steps * b : steps * (b + 2), at]) - count * mean[:, at]
            h = w.astype(jnp.bfloat16)
            e = (w - h.astype(jnp.float32)).astype(jnp.bfloat16)
            hi[out, at] = h
            lo[out, at] = e
            hi_t[at, out] = h.T
            lo_t[at, out] = e.T

    x_copy.wait_recv()

    @pl.when(z == 0)
    def _():
        row = lax.broadcasted_iota(jnp.int32, (pad, pad), 0)
        col = lax.broadcasted_iota(jnp.int32, (pad, pad), 1)
        band = ((col <= row) & (col < length)).astype(jnp.float32).astype(jnp.bfloat16)
        t = lax.broadcasted_iota(jnp.int32, (pad, 1), 0)
        count = jnp.minimum(t + 1, length).astype(jnp.float32)
        for n in range(width // 256):
            at = slice(256 * n, 256 * (n + 1))
            w = dot(band, data[pad : 2 * pad, at]) - count * mean[:, at]
            h = w.astype(jnp.bfloat16)
            e = (w - h.astype(jnp.float32)).astype(jnp.bfloat16)
            hi_e[:, at] = h
            lo_e[:, at] = e
            hi_et[at, :] = h.T
            lo_et[at, :] = e.T
        for p in range(NQ // 2):
            at = pl.ds(pl.multiple_of(half * j + 2 * cols * p, 2 * cols), 2 * cols)
            for r in range(4):
                left = pl.ds(pl.multiple_of(rows * (c ^ r), rows), rows)
                ext[p, r] = (
                    dot(hi_et[left, :], lo_e[:, at])
                    + dot(lo_et[left, :], hi_e[:, at])
                    + dot(hi_et[left, :], hi_e[:, at])
                )

    @pl.when(z != 0)
    def _():
        ext[...] = jnp.zeros_like(ext)

    @pl.when(z > 0)
    def _():
        forwards[0].wait_recv()

    windows(0)

    @pl.when(z < 3)
    def _():
        forwards[1].wait_recv()

    windows(1)

    def send(codes, scales, to_codes, to_scales, sems, at, **where):
        (sc, rc), (ss, rs) = sems
        return [
            copy(codes, to_codes, sc.at[at], rc.at[at], **where),
            copy(scales, to_scales, ss.at[at], rs.at[at], **where),
        ]

    def pack(values, codes, scales, at):
        for g in range(8):
            v = values(g)
            top = jnp.maximum(jnp.max(jnp.abs(v), axis=0, keepdims=True), 1e-33)
            scales[(*at, g // 2, slice(g % 2, g % 2 + 1))] = top * (1.0 / TOP)
            code = jnp.round(v * (TOP / top)).astype(jnp.int32).astype(jnp.int16)
            codes[(*at, slice(32 * g, 32 * g + 32))] = code

    def unpack(codes, scales, at, g, base=None):
        code = codes[(*at, slice(32 * g, 32 * g + 32))].astype(jnp.int32).astype(jnp.float32)
        if base is None:
            return code * scales[(*at, g // 2, slice(g % 2, g % 2 + 1))]
        return code * scales[(*at, slice(g, g + 1))]

    first_hop, second_hop, z_hops, swaps = [], [], [], []
    for q in range(NQ):
        m1 = 1 + q % 2
        m2 = 3 - m1
        first_hop.append([
            send(
                code1.at[q, i], scale1.at[q, i], got1.at[q, i], gots1.at[q, i],
                ((s1, r1), (s1s, r1s)), (q, i), chain=c ^ m1,
            )
            for i in range(2)
        ])
        second_hop.append(
            send(
                code2.at[q], scale2.at[q], got2.at[q], gots2.at[q], ((s2, r2), (s2s, r2s)), q,
                chain=c ^ m2,
            )
        )
        z_hops.append([
            send(
                code3.at[q, pl.ds(pl.multiple_of(zrows * (z ^ s), zrows), zrows), :],
                scale3.at[q, z ^ s], got3.at[q, s - 1], gots3.at[q, s - 1],
                ((s3, r3), (s3s, r3s)), (q, s - 1), tm=k ^ (2 * s),
            )
            for s in range(1, 4)
        ])
        swaps.append(
            copy(
                done.at[q, pl.ds(pl.multiple_of(orows * (1 - j), orows), orows), :],
                other.at[q], s4.at[q], r4.at[q], tm=k ^ 1,
            )
        )

    def hop2(q):
        arrive(first_hop[q][1])
        pack(
            lambda g: keep[q, 1, 32 * g : 32 * g + 32] + unpack(got1, gots1, (q, 1), g),
            code2, scale2, (q,),
        )
        start(second_hop[q])

    def hop3(q):
        arrive(first_hop[q][0])
        arrive(second_hop[q])

        def value(g):
            v = (
                keep[q, 0, 32 * g : 32 * g + 32]
                + unpack(got1, gots1, (q, 0), g)
                + unpack(got2, gots2, (q,), g)
            )
            plane[q, 32 * g : 32 * g + 32] = v
            return v

        pack(value, code3, scale3, (q,))
        for copies in z_hops[q]:
            start(copies)

    def hop4(q):
        for s in range(3):
            arrive(z_hops[q][s])
        for g in range(2):
            at = pl.ds(pl.multiple_of(zrows * z + orows * g, orows), orows)
            here = plane[q, at, :]
            for s in range(3):
                here = here + unpack(got3, gots3, (q, s), g, 0)
            done[q, 32 * g : 32 * g + 32] = here * scale
        swaps[q].start()

    def products(p, go):
        at = pl.ds(pl.multiple_of(half * j + 2 * cols * p, 2 * cols), 2 * cols)
        right_hi = hi[:, at]
        right_lo = lo[:, at]
        for r in (3, 1, 2, 0):
            left = pl.ds(pl.multiple_of(rows * (c ^ r), rows), rows)
            w = (
                dot(hi_t[left, :], right_lo)
                + dot(lo_t[left, :], right_hi)
                + dot(hi_t[left, :], right_hi)
                + ext[p, r]
            )
            for b in range(2):
                q = 2 * p + b
                part = w[:, cols * b : cols * (b + 1)]
                if r == 3 or r == 1 + b:
                    slot = int(r == 3)
                    pack(lambda g: part[32 * g : 32 * g + 32], code1, scale1, (q, slot))
                    if go:
                        start(first_hop[q][slot])
                else:
                    keep[q, int(r != 0)] = part

    products(0, True)
    products(1, False)
    hop2(0)
    hop2(1)
    for i in (1, 0):
        start(first_hop[2][i])
        start(first_hop[3][i])
    hop3(0)
    hop3(1)
    hop2(2)
    hop2(3)
    hop3(2)
    hop3(3)
    for q in range(NQ):
        hop4(q)
    for q in range(NQ):
        o_ref[:, pl.ds(pl.multiple_of(half * j + cols * q, cols), cols)] = done[
            q, pl.ds(pl.multiple_of(orows * j, orows), orows), :
        ]
        swaps[q].wait_recv()
        o_ref[:, pl.ds(pl.multiple_of(half * (1 - j) + cols * q, cols), cols)] = other[q]

    for cp in sum_copies:
        cp.wait_send()
    x_copy.wait_send()

    @pl.when((j == 1) & (z < 3))
    def _():
        for cp in ups:
            cp.wait_send()

    @pl.when((j == 0) & (z > 0))
    def _():
        for cp in downs:
            cp.wait_send()

    @pl.when(z > 0)
    def _():
        forwards[0].wait_send()

    @pl.when(z < 3)
    def _():
        forwards[1].wait_send()

    for q in range(NQ):
        for copies in (*first_hop[q], second_hop[q], *z_hops[q]):
            for cp in copies:
                cp.wait_send()
        swaps[q].wait_send()


def fused(traces, lengths):
    _, steps, width = traces.shape
    f32, bf16, i16 = jnp.float32, jnp.bfloat16, jnp.int16
    rows, cols = width // 4, width // 2 // NQ
    dma = pltpu.SemaphoreType.DMA
    return pl.pallas_call(
        kernel,
        out_shape=jax.ShapeDtypeStruct((width // 32, width), f32),
        in_specs=[
            pl.BlockSpec(memory_space=pltpu.HBM),
            pl.BlockSpec(memory_space=pltpu.HBM),
        ],
        out_specs=pl.BlockSpec(memory_space=pltpu.VMEM),
        scratch_shapes=[
            pltpu.SMEM(lengths.shape, jnp.int32),
            pltpu.VMEM((3 * steps, width), bf16),
            pltpu.VMEM((NQ // 2, 4, rows, 2 * cols), f32),
            pltpu.VMEM((steps // 2, width), bf16),
            pltpu.VMEM((steps // 2, width), bf16),
            pltpu.VMEM((width, steps // 2), bf16),
            pltpu.VMEM((width, steps // 2), bf16),
            pltpu.VMEM((8, 1, width), f32),
            pltpu.VMEM((2 * steps, width), bf16),
            pltpu.VMEM((2 * steps, width), bf16),
            pltpu.VMEM((width, 2 * steps), bf16),
            pltpu.VMEM((width, 2 * steps), bf16),
            pltpu.VMEM((NQ, 2, rows, cols), f32),
            pltpu.VMEM((NQ, 2, rows, cols), i16),
            pltpu.VMEM((NQ, 2, 4, 2, cols), f32),
            pltpu.VMEM((NQ, 2, rows, cols), i16),
            pltpu.VMEM((NQ, 2, 4, 2, cols), f32),
            pltpu.VMEM((NQ, rows, cols), i16),
            pltpu.VMEM((NQ, 4, 2, cols), f32),
            pltpu.VMEM((NQ, rows, cols), i16),
            pltpu.VMEM((NQ, 4, 2, cols), f32),
            pltpu.VMEM((NQ, rows, cols), f32),
            pltpu.VMEM((NQ, rows, cols), i16),
            pltpu.VMEM((NQ, 4, 2, cols), f32),
            pltpu.VMEM((NQ, 3, rows // 4, cols), i16),
            pltpu.VMEM((NQ, 3, 2, cols), f32),
            pltpu.VMEM((NQ, rows // 4, cols), f32),
            pltpu.VMEM((NQ, rows // 8, cols), f32),
            dma((2,)),
            dma((8,)), dma((8,)),
            dma, dma,
            dma((2,)), dma((2,)),
            dma((2,)), dma((2,)),
            dma((NQ, 2)), dma((NQ, 2)), dma((NQ, 2)), dma((NQ, 2)),
            dma((NQ,)), dma((NQ,)), dma((NQ,)), dma((NQ,)),
            dma((NQ, 3)), dma((NQ, 3)), dma((NQ, 3)), dma((NQ, 3)),
            dma((NQ,)), dma((NQ,)),
        ],
        compiler_params=pltpu.CompilerParams(
            collective_id=0, has_side_effects=True, vmem_limit_bytes=67043328
        ),
    )(lengths, traces.reshape(steps, width))


def body(mesh, traces, lengths):
    chains, steps, width = traces.shape
    laid_out = (
        mesh.shape["groups"] == 1 and mesh.shape["chain"] == 4 and mesh.shape["tm"] == 8
    )
    if laid_out and chains == 1 and steps == LAG and width == 1024:
        return fused(traces, lengths)
    return on_device(traces, lengths)


def solution(mesh):
    in_specs = (P(("groups", "chain"), "tm", None), P("groups"))
    out_specs = P(("groups", "chain", "tm"), None)
    return jax.shard_map(
        functools.partial(body, mesh), mesh=mesh, in_specs=in_specs, out_specs=out_specs,
        check_vma=False,
    )
```

```python
import functools

import jax
import jax.numpy as jnp
from jax import lax
from jax.experimental import pallas as pl
from jax.experimental.pallas import tpu as pltpu
from jax.sharding import PartitionSpec as P

LAG = 256
MESH = pl.DeviceIdType.MESH


def shifted(block, axis, distance):
    devices = range(lax.axis_size(axis))
    route = [(i - distance, i) for i in devices if i - distance in devices]
    return lax.ppermute(block, axis, route)


def window_sums(current, previous):
    chains, steps, width = current.shape
    count = steps // LAG
    blocks = current.reshape(chains, count, LAG, width)
    earlier = jnp.concatenate([previous[:, None], blocks[:, :-1]], axis=1)
    index = jnp.arange(LAG)
    lower = index[None, :] <= index[:, None]
    upper = index[None, :] > index[:, None]
    lower_mat = lower.astype(jnp.float32)
    upper_mat = upper.astype(jnp.float32)
    result = jnp.einsum("ij,cbjp->cbip", lower_mat, blocks, precision=lax.Precision.HIGHEST)
    result = result + jnp.einsum(
        "ij,cbjp->cbip", upper_mat, earlier, precision=lax.Precision.HIGHEST
    )
    return result.reshape(chains, steps, width)


def gram_rows(filtered):
    chains, steps, width = filtered.shape
    flat = filtered.reshape(chains * steps, width)
    return jnp.einsum("tk,tp->kp", flat, flat, precision=lax.Precision.HIGHEST)


def on_device(traces, lengths):
    chains, steps, width = traces.shape
    own_len = lax.dynamic_slice_in_dim(lengths, lax.axis_index("chain") * chains, chains)
    first_time = lax.axis_index("tm") * steps
    times = first_time + jnp.arange(steps, dtype=jnp.int32)
    valid = (times[None, :] < own_len[:, None]).astype(jnp.float32)
    back_times = times - steps
    back_valid = ((back_times[None, :] >= 0) & (back_times[None, :] < own_len[:, None])).astype(
        jnp.float32
    )
    behind = shifted(traces, "tm", 1)
    data = traces.astype(jnp.float32) * valid[..., None]
    earlier = behind.astype(jnp.float32) * back_valid[..., None]
    totals = lax.psum(jnp.sum(data, axis=1), "tm")
    mean = totals / own_len.astype(jnp.float32)[:, None]
    scale = 1.0 / (LAG * jnp.sum(lengths).astype(jnp.float32))
    centered = window_sums(
        (data - mean[:, None, :]) * valid[..., None],
        (earlier - mean[:, None, :]) * back_valid[..., None],
    )
    return lax.psum_scatter(
        scale * gram_rows(centered), ("chain", "tm"), scatter_dimension=0, tiled=True
    )


def dot(a, b):
    return jnp.dot(a, b, preferred_element_type=jnp.float32)


NQ = 4
TOP = 32767.0


def kernel(
    len_hbm, x_hbm, o_ref, len_ref, data, ext, hi_e, lo_e, hi_et, lo_et, sums, hi, lo, hi_t, lo_t, keep, code1, scale1, got1,
    gots1, code2, scale2, got2, gots2, plane, code3, scale3, got3, gots3, in_sem, s_sum, r_sum, s_x, r_x,
    s_halo, r_halo, s_fwd, r_fwd, s1, r1, s1s,
    r1s, s2, r2, s2s, r2s, s3, r3, s3s, r3s,
):
    steps, width = x_hbm.shape
    pad = steps // 2
    half = width // 2
    cols = half // NQ
    rows = width // 4
    orows = rows // 8
    c = lax.axis_index("chain")
    k = lax.axis_index("tm")
    z = k // 2
    j = k % 2

    def copy(src, dst, send, recv, **where):
        return pltpu.make_async_remote_copy(
            src_ref=src, dst_ref=dst, send_sem=send, recv_sem=recv, device_id=where,
            device_id_type=MESH,
        )

    def start(copies):
        for cp in copies:
            cp.start()

    def arrive(copies):
        for cp in copies:
            cp.wait_recv()

    own = pl.ds(pl.multiple_of(pad + steps * j, pad), steps)
    len_in = pltpu.make_async_copy(len_hbm, len_ref, in_sem.at[0])
    x_in = pltpu.make_async_copy(x_hbm, data.at[own, :], in_sem.at[1])
    len_in.start()
    x_in.start()
    barrier = pltpu.get_barrier_semaphore()
    for r in range(1, 8):
        pl.semaphore_signal(barrier, inc=1, device_id={"tm": k ^ r}, device_id_type=MESH)
    for r in (1, 2):
        pl.semaphore_signal(barrier, inc=1, device_id={"chain": c ^ r}, device_id_type=MESH)

    len_in.wait()
    length = len_ref[c]
    total_len = len_ref[0]
    for i in range(1, len_ref.shape[0]):
        total_len = total_len + len_ref[i]
    scale = 1.0 / (LAG * jnp.full((1, 1), total_len, jnp.int32).astype(jnp.float32))

    time = k * steps + lax.broadcasted_iota(jnp.int32, (steps, 1), 0)
    valid = (time < length).astype(jnp.float32)
    x_in.wait()
    sums[0] = jnp.sum(data[own, :].astype(jnp.float32) * valid, axis=0, keepdims=True)

    @pl.when(z == 0)
    def _():
        data[0:pad, :] = jnp.zeros((pad, width), data.dtype)

    @pl.when(z == 3)
    def _():
        data[5 * pad : 6 * pad, :] = jnp.zeros((pad, width), data.dtype)

    pl.semaphore_wait(barrier, 9)

    sum_copies = [
        copy(sums.at[0], sums.at[r], s_sum.at[r], r_sum.at[r], tm=k ^ r) for r in range(1, 8)
    ]
    for cp in sum_copies:
        cp.start()
    def halo(way, h):
        near = 2 * jnp.minimum(z + 1, 3) if way == 0 else 2 * jnp.maximum(z - 1, 0)
        take = 4 * pad if way == 0 else pad
        put = 0 if way == 0 else 5 * pad
        at = pl.ds(half * h, half)
        return copy(
            data.at[pl.ds(take, pad), at], data.at[pl.ds(put, pad), at], s_halo.at[h],
            r_halo.at[way], tm=near + h,
        )

    ups = [halo(0, h) for h in range(2)]
    downs = [halo(1, h) for h in range(2)]

    @pl.when((j == 1) & (z < 3))
    def _():
        start(ups)

    @pl.when((j == 0) & (z > 0))
    def _():
        start(downs)

    x_copy = copy(data.at[own, :], data.at[own, :], s_x, r_x, tm=k ^ 1)
    x_copy.start()

    mine = pl.ds(pl.multiple_of(half * j, half), half)
    forwards, landed = [], []
    for way, put in ((0, 0), (1, 5 * pad)):
        block = data.at[pl.ds(put, pad), mine]
        forwards.append(copy(block, block, s_fwd.at[way], r_fwd.at[way], tm=k ^ 1))
        landed.append(copy(block, block, s_halo.at[0], r_halo.at[way], tm=k ^ 1))

    @pl.when(z > 0)
    def _():
        landed[0].wait_recv()
        forwards[0].start()

    @pl.when(z < 3)
    def _():
        landed[1].wait_recv()
        forwards[1].start()

    i_idx = lax.broadcasted_iota(jnp.int32, (steps, 2 * steps), 0)
    r_idx = lax.broadcasted_iota(jnp.int32, (steps, 2 * steps), 1)
    for cp in sum_copies:
        cp.wait_recv()
    total = sums[0]
    for r in range(1, 8):
        total = total + sums[r]
    mean = total / jnp.full((1, 1), length, jnp.int32).astype(jnp.float32)

    def windows(b):
        first = 2 * steps * z + pad + steps * b
        when = first - steps + r_idx
        keep = (r_idx > i_idx) & (r_idx <= i_idx + LAG) & (when >= 0) & (when < length)
        band = keep.astype(jnp.float32).astype(jnp.bfloat16)
        t = first + lax.broadcasted_iota(jnp.int32, (steps, 1), 0)
        count = jnp.maximum(
            jnp.minimum(t + 1, length) - jnp.maximum(t - (LAG - 1), 0), 0
        ).astype(jnp.float32)
        out = slice(steps * b, steps * (b + 1))
        for n in range(width // 256):
            at = slice(256 * n, 256 * (n + 1))
            w = dot(band, data[steps * b : steps * (b + 2), at]) - count * mean[:, at]
            h = w.astype(jnp.bfloat16)
            e = (w - h.astype(jnp.float32)).astype(jnp.bfloat16)
            hi[out, at] = h
            lo[out, at] = e
            hi_t[at, out] = h.T
            lo_t[at, out] = e.T

    x_copy.wait_recv()

    @pl.when(z == 0)
    def _():
        row = lax.broadcasted_iota(jnp.int32, (pad, pad), 0)
        col = lax.broadcasted_iota(jnp.int32, (pad, pad), 1)
        band = ((col <= row) & (col < length)).astype(jnp.float32).astype(jnp.bfloat16)
        t = lax.broadcasted_iota(jnp.int32, (pad, 1), 0)
        count = jnp.minimum(t + 1, length).astype(jnp.float32)
        for n in range(width // 256):
            at = slice(256 * n, 256 * (n + 1))
            w = dot(band, data[pad : 2 * pad, at]) - count * mean[:, at]
            h = w.astype(jnp.bfloat16)
            e = (w - h.astype(jnp.float32)).astype(jnp.bfloat16)
            hi_e[:, at] = h
            lo_e[:, at] = e
            hi_et[at, :] = h.T
            lo_et[at, :] = e.T
        for p in range(NQ // 2):
            at = pl.ds(pl.multiple_of(half * j + 2 * cols * p, 2 * cols), 2 * cols)
            for r in range(4):
                left = pl.ds(pl.multiple_of(rows * (c ^ r), rows), rows)
                ext[p, r] = (
                    dot(hi_et[left, :], lo_e[:, at])
                    + dot(lo_et[left, :], hi_e[:, at])
                    + dot(hi_et[left, :], hi_e[:, at])
                )

    @pl.when(z != 0)
    def _():
        ext[...] = jnp.zeros_like(ext)

    @pl.when(z > 0)
    def _():
        forwards[0].wait_recv()

    windows(0)

    @pl.when(z < 3)
    def _():
        forwards[1].wait_recv()

    windows(1)

    def send(codes, scales, to_codes, to_scales, sems, at, **where):
        (sc, rc), (ss, rs) = sems
        return [
            copy(codes, to_codes, sc.at[at], rc.at[at], **where),
            copy(scales, to_scales, ss.at[at], rs.at[at], **where),
        ]

    def pack(values, codes, scales, at, flat=False):
        for g in range(8):
            v = values(g)
            top = jnp.maximum(jnp.max(jnp.abs(v), axis=0, keepdims=True), 1e-33)
            place = (g,) if flat else (g // 2, slice(g % 2, g % 2 + 1))
            scales[(*at, *place)] = top * (1.0 / TOP)
            code = jnp.round(v * (TOP / top)).astype(jnp.int32).astype(jnp.int16)
            codes[(*at, slice(32 * g, 32 * g + 32))] = code

    def unpack(codes, scales, at, g):
        code = codes[(*at, slice(32 * g, 32 * g + 32))].astype(jnp.int32).astype(jnp.float32)
        return code * scales[(*at, g // 2, slice(g % 2, g % 2 + 1))]

    first_hop, second_hop, z_hops = [], [], []

    def goal(i):
        return k ^ i

    for q in range(NQ):
        m1 = 1 + q % 2
        m2 = 3 - m1
        first_hop.append([
            send(
                code1.at[q, i], scale1.at[q, i], got1.at[q, i], gots1.at[q, i],
                ((s1, r1), (s1s, r1s)), (q, i), chain=c ^ m1,
            )
            for i in range(2)
        ])
        second_hop.append(
            send(
                code2.at[q], scale2.at[q], got2.at[q], gots2.at[q], ((s2, r2), (s2s, r2s)), q,
                chain=c ^ m2,
            )
        )
        z_hops.append([
            send(
                code3.at[q, pl.ds(pl.multiple_of(goal(i) * orows, orows), orows), :],
                scale3.at[q, goal(i)], got3.at[q, i - 1], gots3.at[q, i - 1],
                ((s3, r3), (s3s, r3s)), (q, i - 1), tm=k ^ i,
            )
            for i in range(1, 8)
        ])

    def hop2(q):
        arrive(first_hop[q][1])
        pack(
            lambda g: keep[q, 1, 32 * g : 32 * g + 32] + unpack(got1, gots1, (q, 1), g),
            code2, scale2, (q,),
        )
        start(second_hop[q])

    def hop3(q):
        arrive(first_hop[q][0])
        arrive(second_hop[q])

        def value(g):
            v = (
                keep[q, 0, 32 * g : 32 * g + 32]
                + unpack(got1, gots1, (q, 0), g)
                + unpack(got2, gots2, (q,), g)
            )
            plane[q, 32 * g : 32 * g + 32] = v
            return v

        pack(value, code3, scale3, (q,), True)
        for copies in z_hops[q]:
            start(copies)

    def hop4(q):
        here = plane[q, pl.ds(pl.multiple_of(orows * k, orows), orows), :]
        there = None
        for i in (2, 4, 6, 1, 3, 5, 7):
            arrive(z_hops[q][i - 1])
            v = got3[q, i - 1].astype(jnp.int32).astype(jnp.float32) * gots3[q, i - 1]
            if i % 2 == 0:
                here = here + v
            else:
                there = v if there is None else there + v
        o_ref[:, pl.ds(pl.multiple_of(half * j + cols * q, cols), cols)] = here * scale
        o_ref[:, pl.ds(pl.multiple_of(half * (1 - j) + cols * q, cols), cols)] = there * scale

    def products(p, go):
        at = pl.ds(pl.multiple_of(half * j + 2 * cols * p, 2 * cols), 2 * cols)
        right_hi = hi[:, at]
        right_lo = lo[:, at]
        for r in (3, 1, 2, 0):
            left = pl.ds(pl.multiple_of(rows * (c ^ r), rows), rows)
            w = (
                dot(hi_t[left, :], right_lo)
                + dot(lo_t[left, :], right_hi)
                + dot(hi_t[left, :], right_hi)
                + ext[p, r]
            )
            for b in range(2):
                q = 2 * p + b
                part = w[:, cols * b : cols * (b + 1)]
                if r == 3 or r == 1 + b:
                    slot = int(r == 3)
                    pack(lambda g: part[32 * g : 32 * g + 32], code1, scale1, (q, slot))
                    if go:
                        start(first_hop[q][slot])
                else:
                    keep[q, int(r != 0)] = part

    products(0, True)
    products(1, False)
    hop2(0)
    hop2(1)
    for i in (1, 0):
        start(first_hop[2][i])
        start(first_hop[3][i])
    hop3(0)
    hop3(1)
    hop2(2)
    hop2(3)
    hop3(2)
    hop3(3)
    for q in range(NQ):
        hop4(q)
    for cp in sum_copies:
        cp.wait_send()
    x_copy.wait_send()

    @pl.when((j == 1) & (z < 3))
    def _():
        for cp in ups:
            cp.wait_send()

    @pl.when((j == 0) & (z > 0))
    def _():
        for cp in downs:
            cp.wait_send()

    @pl.when(z > 0)
    def _():
        forwards[0].wait_send()

    @pl.when(z < 3)
    def _():
        forwards[1].wait_send()

    for q in range(NQ):
        for copies in (*first_hop[q], second_hop[q], *z_hops[q]):
            for cp in copies:
                cp.wait_send()


def fused(traces, lengths):
    _, steps, width = traces.shape
    f32, bf16, i16 = jnp.float32, jnp.bfloat16, jnp.int16
    rows, cols = width // 4, width // 2 // NQ
    dma = pltpu.SemaphoreType.DMA
    return pl.pallas_call(
        kernel,
        out_shape=jax.ShapeDtypeStruct((width // 32, width), f32),
        in_specs=[
            pl.BlockSpec(memory_space=pltpu.HBM),
            pl.BlockSpec(memory_space=pltpu.HBM),
        ],
        out_specs=pl.BlockSpec(memory_space=pltpu.VMEM),
        scratch_shapes=[
            pltpu.SMEM(lengths.shape, jnp.int32),
            pltpu.VMEM((3 * steps, width), bf16),
            pltpu.VMEM((NQ // 2, 4, rows, 2 * cols), f32),
            pltpu.VMEM((steps // 2, width), bf16),
            pltpu.VMEM((steps // 2, width), bf16),
            pltpu.VMEM((width, steps // 2), bf16),
            pltpu.VMEM((width, steps // 2), bf16),
            pltpu.VMEM((8, 1, width), f32),
            pltpu.VMEM((2 * steps, width), bf16),
            pltpu.VMEM((2 * steps, width), bf16),
            pltpu.VMEM((width, 2 * steps), bf16),
            pltpu.VMEM((width, 2 * steps), bf16),
            pltpu.VMEM((NQ, 2, rows, cols), f32),
            pltpu.VMEM((NQ, 2, rows, cols), i16),
            pltpu.VMEM((NQ, 2, 4, 2, cols), f32),
            pltpu.VMEM((NQ, 2, rows, cols), i16),
            pltpu.VMEM((NQ, 2, 4, 2, cols), f32),
            pltpu.VMEM((NQ, rows, cols), i16),
            pltpu.VMEM((NQ, 4, 2, cols), f32),
            pltpu.VMEM((NQ, rows, cols), i16),
            pltpu.VMEM((NQ, 4, 2, cols), f32),
            pltpu.VMEM((NQ, rows, cols), f32),
            pltpu.VMEM((NQ, rows, cols), i16),
            pltpu.VMEM((NQ, 8, 1, cols), f32),
            pltpu.VMEM((NQ, 7, rows // 8, cols), i16),
            pltpu.VMEM((NQ, 7, 1, cols), f32),
            dma((2,)),
            dma((8,)), dma((8,)),
            dma, dma,
            dma((2,)), dma((2,)),
            dma((2,)), dma((2,)),
            dma((NQ, 2)), dma((NQ, 2)), dma((NQ, 2)), dma((NQ, 2)),
            dma((NQ,)), dma((NQ,)), dma((NQ,)), dma((NQ,)),
            dma((NQ, 7)), dma((NQ, 7)), dma((NQ, 7)), dma((NQ, 7)),
        ],
        compiler_params=pltpu.CompilerParams(
            collective_id=0, has_side_effects=True, vmem_limit_bytes=67043328
        ),
    )(lengths, traces.reshape(steps, width))


def body(mesh, traces, lengths):
    chains, steps, width = traces.shape
    laid_out = (
        mesh.shape["groups"] == 1 and mesh.shape["chain"] == 4 and mesh.shape["tm"] == 8
    )
    if laid_out and chains == 1 and steps == LAG and width == 1024:
        return fused(traces, lengths)
    return on_device(traces, lengths)


def solution(mesh):
    in_specs = (P(("groups", "chain"), "tm", None), P("groups"))
    out_specs = P(("groups", "chain", "tm"), None)
    return jax.shard_map(
        functools.partial(body, mesh), mesh=mesh, in_specs=in_specs, out_specs=out_specs,
        check_vma=False,
    )
```
